32 devices in a mesh: lat: 4 (over x, core), src: 8 (over z, y).
Axes of the slice: x: 2, y: 2, z: 4, core: 2. Of those that a mesh axis runs over, the one named last changes fastest.
Arguments:
- fine_residual: bfloat16 [8, 16, 256, 2048], P('lat', 'src'), may hold values from -6 to 6
- basis: bfloat16 [8, 16, 2048, 128], P('lat', 'src'), may hold values from -0.25 to 0.25
- diag_inverse: bfloat16 [8, 16, 128, 128], P('lat', 'src'), may hold values from -0.32 to 1.7, as said below
- hoppings: bfloat16 [8, 16, 8, 128, 128], P('lat', 'src'), may hold values from -0.125 to 0.125
- neighbours: int32 [16, 6], replicated, may hold values from 0 to 15, as said below
- aggregation: int32 [8, 16], P('lat', 'src'), may hold values from 0 to 15, as said below
Outputs:
- correction: bfloat16 [8, 16, 256, 2048], P('lat', 'src')
The draws below stay inside these ranges and needn't reach their ends.
Inputs may be any that keep to these rules, and one draw needn't show every extreme that they name: `diag_inverse`: a site's diagonal inverse is one on the diagonal within a fifth (two fifths in some draws) plus independent off-diagonal entries. The spatial sites form a periodic grid of 8 by 1 by 2 sites, site (x, y, z) having index (x * 1 + y) * 2 + z; columns 2k and 2k+1 hold the two periodic neighbours along grid direction k, one step up and one step down, in an order drawn for each k. `aggregation`: in each row, every aligned block of 2 entries is a permutation of that block's own column indices.
All inputs are finite; a program needn't handle non-finite values.
Results may differ from the reference program's by a relative error of at most 0.0075.
Values may be sent and summed in bfloat16 or wider, within the bound.
A program may use at most 128 MiB of HBM per device.

```python
import math
import jax
import jax.numpy as jnp
from jax import lax

FINE = 2048
CDOF = 128
NSRC = 256
SWEEPS = 3
SP_DEV = 2
NT = 8
SPACE = 16


def draw_diag_inverse(key, part):
    first_key, second_key = jax.random.split(key)
    identity = jnp.eye(CDOF, dtype=jnp.float32)
    off_diag = jnp.clip(jax.random.normal(first_key, (NT, SPACE, CDOF, CDOF), jnp.float32) * (0.5 / math.sqrt(CDOF)), -0.3, 0.3)
    diag_part = jax.random.uniform(second_key, (NT, SPACE, 1, 1), jnp.float32, 0.8, 1.2)
    return (off_diag * (1.0 - identity) + diag_part * identity).astype(jnp.bfloat16)


def grid_index(x_pos, y_pos, z_pos, y_len):
    return ((x_pos * y_len + y_pos) * 2 + z_pos).astype(jnp.int32)


def draw_neighbours(key, part):
    flips = jax.random.randint(jax.random.fold_in(key, 17), (3,), 0, 2).astype(jnp.int32)
    x_len = SPACE // SP_DEV
    y_len = SP_DEV // 2
    sites = jnp.arange(SPACE, dtype=jnp.int32)
    z_pos = sites % 2
    y_pos = sites // 2 % y_len
    x_pos = sites // SP_DEV
    pairs = [(grid_index((x_pos + 1) % x_len, y_pos, z_pos, y_len), grid_index((x_pos + x_len - 1) % x_len, y_pos, z_pos, y_len)), (grid_index(x_pos, (y_pos + 1) % y_len, z_pos, y_len), grid_index(x_pos, (y_pos + y_len - 1) % y_len, z_pos, y_len)), (grid_index(x_pos, y_pos, (z_pos + 1) % 2, y_len), grid_index(x_pos, y_pos, (z_pos + 1) % 2, y_len))]
    columns = []
    for direction in range(3):
        upward, downward = pairs[direction]
        flipped = flips[direction] == 1
        columns.append(jnp.where(flipped, downward, upward))
        columns.append(jnp.where(flipped, upward, downward))
    return jnp.stack(columns, axis=1).astype(jnp.int32)


def draw_aggregation(key, part):
    blocks = SPACE // SP_DEV
    subkeys = jax.random.split(key, NT * blocks)
    within = jax.vmap(lambda single: jax.random.permutation(single, SP_DEV))(subkeys).astype(jnp.int32)
    offsets = jnp.arange(NT * blocks, dtype=jnp.int32) % blocks * SP_DEV
    return (within + offsets[:, None]).reshape(NT, SPACE)


def block_scale(key, dims, shards, least, largest):
    gain = 1.0
    for axis_at, shards_of in shards:
        draws = jax.random.uniform(jax.random.fold_in(jax.random.fold_in(key, 6), axis_at), (shards_of,), jnp.float32, least / len(shards), largest / len(shards))
        gain = gain * jnp.repeat(jnp.exp(draws), dims[axis_at] // shards_of).reshape((-1,) + (1,) * (len(dims) - 1 - axis_at))
    return gain


def noise(key, dims, deviation, bound, cuts=(), held_as=jnp.bfloat16):
    entries = jax.random.normal(key, dims, jnp.float32) * deviation
    if len(cuts) > 0:
        entries = block_scale(key, dims, cuts, -0.22, 0.18) * entries
    return jnp.clip(entries, min=-bound, max=bound).astype(held_as)


def setup_inputs(seed: int = 0) -> dict:
    streams_of = jax.random.split(jax.random.key(seed), 7)
    return {
        "fine_residual": noise(streams_of[0], (NT, SPACE, NSRC, FINE), 1.0, 6.0, ((0, 4), (1, 8))),
        "basis": noise(streams_of[1], (NT, SPACE, FINE, CDOF), (FINE // 4) ** -0.5, 0.25, ((0, 4), (1, 8))),
        "diag_inverse": draw_diag_inverse(jax.random.fold_in(streams_of[6], 71), 0),
        "hoppings": noise(streams_of[3], (NT, SPACE, 8, CDOF, CDOF), (16 * CDOF) ** -0.5, 0.125, ((0, 4), (1, 8))),
        "neighbours": draw_neighbours(jax.random.fold_in(streams_of[6], 71), 0),
        "aggregation": draw_aggregation(jax.random.fold_in(streams_of[6], 71), 0),
    }


damping = 0.8


def hop_sum(iterate, hoppings, neighbours, slices):
    def per_slice(slice_index):
        current = iterate[slice_index]
        spatial = jnp.take(current, neighbours, axis=0)
        upper_time = iterate[(slice_index + 1) % NT]
        lower_time = iterate[(slice_index + NT - 1) % NT]
        stacked = jnp.concatenate([spatial, upper_time[:, None], lower_time[:, None]], axis=1).astype(jnp.float32)
        return jnp.einsum('sknc,skcd->snd', stacked, hoppings[slice_index].astype(jnp.float32))
    return lax.map(per_slice, slices)


def reference(fine_residual, basis, diag_inverse, hoppings, neighbours, aggregation):
    slices = jnp.arange(NT, dtype=jnp.int32)

    def restrict_slice(slice_index):
        return jnp.einsum('snr,src->snc', fine_residual[slice_index].astype(jnp.float32), basis[slice_index].astype(jnp.float32)).astype(jnp.bfloat16)

    restricted = lax.map(restrict_slice, slices)
    inverse = jnp.argsort(aggregation, axis=1).astype(jnp.int32)
    coarse_rhs = jnp.take_along_axis(restricted, inverse[:, :, None, None], axis=1)
    inverse_blocks = diag_inverse.astype(jnp.float32)
    applied = jnp.einsum('tsnc,tscd->tsnd', coarse_rhs.astype(jnp.float32), inverse_blocks)
    iterate = (damping * applied).astype(jnp.bfloat16)
    for sweep_index in range(SWEEPS - 1):
        hop_terms = hop_sum(iterate, hoppings, neighbours, slices)
        difference = (coarse_rhs.astype(jnp.float32) - hop_terms).astype(jnp.bfloat16)
        applied = jnp.einsum('tsnc,tscd->tsnd', difference.astype(jnp.float32), inverse_blocks)
        iterate = ((1.0 - damping) * iterate.astype(jnp.float32) + damping * applied).astype(jnp.bfloat16)
    gathered = jnp.take_along_axis(iterate, aggregation[:, :, None, None], axis=1)

    def prolong_slice(slice_index):
        return jnp.einsum('snc,src->snr', gathered[slice_index].astype(jnp.float32), basis[slice_index].astype(jnp.float32)).astype(jnp.bfloat16)

    return lax.map(prolong_slice, slices)
```

```python
import functools
import math

import jax
import jax.numpy as jnp
from jax import lax
from jax.experimental import pallas as pl
from jax.experimental.pallas import tpu as pltpu
from jax.sharding import PartitionSpec as P

SWEEPS = 3
DAMPING = 0.8
CHUNKS = 4
BLOCKS = (1, 1, 2)
VMEM_BYTES = 67043328
CROSS_BLOCK = 1
HEAD = 2
FORWARD_AT = (0.0, 5.0)
FINISH_AT = (2.4, 7.4)
LOCAL_AT = (-1.0, 2.5)
F32 = jnp.float32
BF16 = jnp.bfloat16


def dot(a, b):
    return jnp.dot(a, b, preferred_element_type=F32)


def timetable(times, sites):
    steps = []
    for c in range(CHUNKS):
        for x in range(SWEEPS - 1):
            steps.append((FORWARD_AT[x] + c, 0, "forward", x, c))
            steps.append((LOCAL_AT[x] + c, 1, "local", x, c))
            steps.append((FINISH_AT[x] + c, 2, "finish", x, c))
    count = times * sites
    for n in range(count):
        steps.append((FINISH_AT[-1] + HEAD - 1 + n * (CHUNKS - HEAD) / count, 3, "prolong", n // sites, n % sites))
    return [step[2:] for step in sorted(steps)]


def sweep_kernel(
    lats, srcs, fine, basis, diag, hops, table_h, agg_h, last, basis_v, out_v,
    table, agg, table_sem, agg_sem, fine_v, diag_v, hops_v, rhs, acc, cells, from_partner, from_far, above, below,
    fine_sem, basis_sem, diag_sem, hops_sem,
    partner_send, partner_recv, far_send, far_recv, above_send, above_recv, below_send, below_recv,
    far_ready, cross_ready,
):
    times, sites, sources, _ = fine.shape
    width = basis.shape[3]
    rows = sources // CHUNKS
    lat, src = lax.axis_index("lat"), lax.axis_index("src")
    later, earlier = lax.rem(lat + 1, lats), lax.rem(lat + lats - 1, lats)
    odd = lax.rem(src, 2)
    partner = src + 1 - 2 * odd
    far_target = lax.rem(src + 2 - 4 * odd + srcs, srcs)
    mate = lat + 1 - 2 * lax.rem(lat, 2)
    cross = lax.rem(lat - 1 + 2 * lax.rem(lat, 2) + lats, lats)
    up, down = lax.rem(src + 2, srcs), lax.rem(src - 2 + srcs, srcs)
    first_of_cross = lat < cross
    barrier = pltpu.get_barrier_semaphore()

    def signal(semaphore, device):
        pl.semaphore_signal(semaphore, inc=1, device_id=device, device_id_type=pl.DeviceIdType.MESH)

    signal(barrier, (lat, down))
    signal(barrier, (lat, partner))
    signal(barrier, (mate, src))

    def meet():
        pl.semaphore_wait(barrier, jnp.where(first_of_cross, 3, 4))

        @pl.when(odd == 1)
        def _():
            signal(far_ready, (lat, up))

        @pl.when(jnp.logical_not(first_of_cross))
        def _():
            signal(cross_ready, (cross, src))

    spans = []
    for b, n in enumerate(BLOCKS):
        spans.append((sum(BLOCKS[:b]), n))

    def load_fine(b, t, s):
        first, n = spans[b]
        span = pl.ds(first * rows, n * rows)
        return pltpu.make_async_copy(fine.at[t, s, span], fine_v.at[t, s, span], fine_sem.at[b, t, s])

    def load_basis(t, s):
        return pltpu.make_async_copy(basis.at[t, s], basis_v.at[t, s], basis_sem.at[t, s])

    load_table = pltpu.make_async_copy(table_h, table, table_sem)
    load_agg = pltpu.make_async_copy(agg_h, agg, agg_sem)
    load_diag = pltpu.make_async_copy(diag, diag_v, diag_sem)
    load_hops = pltpu.make_async_copy(hops, hops_v, hops_sem)

    def start_block(b):
        for t in range(times):
            for s in range(sites):
                if b == 0:
                    load_basis(t, s).start()
                load_fine(b, t, s).start()
            if b == 0 and t == 0:
                load_diag.start()

    start_block(0)
    load_agg.start()
    load_table.start()

    @pl.when(first_of_cross)
    def _():
        signal(barrier, (cross, src))

    for b in range(1, len(BLOCKS)):
        start_block(b)
        if b == 1:
            load_hops.start()

    def remote(source, target, send, recv, device):
        return pltpu.make_async_remote_copy(
            src_ref=source, dst_ref=target, send_sem=send, recv_sem=recv,
            device_id=device, device_id_type=pl.DeviceIdType.MESH)

    def to_partner(x, c):
        return remote(cells.at[x, c], from_partner.at[x, c],
                      partner_send.at[x, c], partner_recv.at[x, c], (lat, partner))

    def to_far(x, c):
        return remote(from_partner.at[x, c], from_far.at[x, c],
                      far_send.at[x, c], far_recv.at[x, c], (lat, far_target))

    def to_later(x, c):
        return remote(cells.at[x, c, times - 1], below.at[x, c],
                      below_send.at[x, c], below_recv.at[x, c], (later, src))

    def to_earlier(x, c):
        return remote(cells.at[x, c, 0], above.at[x, c],
                      above_send.at[x, c], above_recv.at[x, c], (earlier, src))

    def send_time(x, c):
        to_later(x, c).start()
        to_earlier(x, c).start()

    def exchanged(t, values):
        swap = lax.rem(agg[t, 0], sites) == 1
        return [jnp.where(swap, values[1 - s], values[s]) for s in range(sites)]

    def restrict(b):
        first, n = spans[b]
        span = pl.ds(first * rows, n * rows)
        for t in range(times):
            for s in range(sites):
                if b == 0:
                    load_basis(t, s).wait()
                load_fine(b, t, s).wait()
        if b == 0:
            load_diag.wait()
            load_agg.wait()
        coarse = [[dot(fine_v[t, s, span], basis_v[t, s]) for s in range(sites)] for t in range(times)]
        here = [exchanged(t, [value.astype(BF16) for value in coarse[t]]) for t in range(times)]
        applied = [[dot(here[t][s], diag_v[t, s]) for s in range(sites)] for t in range(times)]
        for t in range(times):
            for s in range(sites):
                start = (DAMPING * applied[t][s]).astype(BF16)
                for i in range(n):
                    part = slice(i * rows, (i + 1) * rows)
                    cells[0, first + i, t, s] = start[part]
                    rhs[first + i, t, s] = here[t][s][part]
        if b == 0:
            meet()
        for i in range(n):
            to_partner(0, first + i).start()

    sent = 0
    for b in range(len(BLOCKS)):
        restrict(b)
        if b == CROSS_BLOCK:

            @pl.when(first_of_cross)
            def _():
                pl.semaphore_wait(cross_ready, 1)

        if b >= CROSS_BLOCK:
            for c in range(sent, spans[b][0] + spans[b][1]):
                send_time(0, c)
            sent = spans[b][0] + spans[b][1]
    load_table.wait()
    load_hops.wait()

    partner_first = [table[0, src * sites + s] == partner * sites + s for s in range(sites)]

    def local(x, c):
        for t in range(times):
            for s in range(sites):
                own, other = cells[x, c, t, s], cells[x, c, t, 1 - s]
                total = dot(jnp.concatenate([own, own], axis=1), hops_v[t, s, 2:4].reshape(-1, width))
                total += dot(jnp.concatenate([other, other], axis=1), hops_v[t, s, 4:6].reshape(-1, width))
                if t + 1 < times:
                    total += dot(cells[x, c, t + 1, s], hops_v[t, s, 6])
                if t > 0:
                    total += dot(cells[x, c, t - 1, s], hops_v[t, s, 7])
                acc[c, t, s] = rhs[c, t, s].astype(F32) - total

    def forward(x, c):
        to_partner(x, c).wait_recv()
        if x == 0 and c == 0:

            @pl.when(odd == 1)
            def _():
                pl.semaphore_wait(far_ready, 1)

        to_far(x, c).start()

    def finish(x, c):
        to_earlier(x, c).wait_recv()
        to_later(x, c).wait_recv()
        to_far(x, c).wait_recv()
        blocks = [(t, s) for t in range(times) for s in range(sites)]
        totals = {}
        for t, s in blocks:
            near, far = from_partner[x, c, t, s], from_far[x, c, t, s]
            pair = jnp.concatenate(
                [jnp.where(partner_first[s], near, far), jnp.where(partner_first[s], far, near)], axis=1)
            totals[t, s] = dot(pair, hops_v[t, s, 0:2].reshape(-1, width))
            if t == times - 1:
                totals[t, s] += dot(above[x, c, s], hops_v[t, s, 6])
            if t == 0:
                totals[t, s] += dot(below[x, c, s], hops_v[t, s, 7])
        differences = {(t, s): (acc[c, t, s] - totals[t, s]).astype(BF16) for t, s in blocks}
        applied = {(t, s): dot(differences[t, s], diag_v[t, s]) for t, s in blocks}
        new = {
            (t, s): ((1.0 - DAMPING) * cells[x, c, t, s].astype(F32) + DAMPING * applied[t, s]).astype(BF16)
            for t, s in blocks
        }
        if x + 1 < SWEEPS - 1:
            for t in range(times):
                for s in range(sites):
                    cells[x + 1, c, t, s] = new[t, s]
            to_partner(x + 1, c).start()
            send_time(x + 1, c)
        else:
            for t in range(times):
                gathered = exchanged(t, [new[t, s] for s in range(sites)])
                for s in range(sites):
                    last[t, s, pl.ds(c * rows, rows)] = gathered[s]

    def prolong(t, s):
        span = pl.ds(0, HEAD * rows)
        out_v[t, s, span] = lax.dot_general(
            last[t, s, span], basis_v[t, s], (((1,), (1,)), ((), ())), preferred_element_type=F32).astype(BF16)

    actions = {"forward": forward, "local": local, "finish": finish, "prolong": prolong}
    for name, *at in timetable(times, sites):
        actions[name](*at)

    for c in range(CHUNKS):
        for x in range(SWEEPS - 1):
            to_partner(x, c).wait_send()
            to_far(x, c).wait_send()
            to_later(x, c).wait_send()
            to_earlier(x, c).wait_send()


def prolong_kernel(cells, basis, head_v, out, tail_v, head_sem, tail_sem):
    times, sites, sources, _ = cells.shape
    top = HEAD * (sources // CHUNKS)
    head, tail = pl.ds(0, top), pl.ds(top, sources - top)
    blocks = [(t, s) for t in range(times) for s in range(sites)]

    def store_head(t, s):
        return pltpu.make_async_copy(head_v.at[t, s, head], out.at[t, s, head], head_sem.at[t, s])

    def store_tail(t, s):
        return pltpu.make_async_copy(tail_v.at[t, s], out.at[t, s, tail], tail_sem.at[t, s])

    for t, s in blocks:
        store_head(t, s).start()
    for t, s in blocks:
        tail_v[t, s] = lax.dot_general(
            cells[t, s, tail], basis[t, s], (((1,), (1,)), ((), ())), preferred_element_type=F32).astype(BF16)
        store_tail(t, s).start()
    for t, s in blocks:
        store_head(t, s).wait()
        store_tail(t, s).wait()


def body(lats, srcs, fine, basis, diag, hops, table, agg):
    times, sites, sources, depth = fine.shape
    width = basis.shape[3]
    exchanges = SWEEPS - 1
    rows = sources // CHUNKS
    any_spec = pl.BlockSpec(memory_space=pl.ANY)
    vmem_spec = pl.BlockSpec(memory_space=pltpu.VMEM)
    dma = pltpu.SemaphoreType.DMA
    piece = (times, sites, rows, width)
    per_chunk = dma((exchanges, CHUNKS))
    handed = 2 * (times * sites * sources * width + math.prod(basis.shape) + math.prod(fine.shape))
    grant = VMEM_BYTES - handed - 2**18
    cells, basis, head = pl.pallas_call(
        functools.partial(sweep_kernel, lats, srcs),
        out_shape=[
            pltpu.VMEM((times, sites, sources, width), BF16),
            pltpu.VMEM(basis.shape, BF16),
            pltpu.VMEM(fine.shape, BF16),
        ],
        in_specs=[any_spec] * 6,
        out_specs=[vmem_spec] * 3,
        scratch_shapes=[
            pltpu.SMEM(table.shape[::-1], jnp.int32),
            pltpu.SMEM(agg.shape, jnp.int32),
            dma(()),
            dma(()),
            pltpu.VMEM(fine.shape, BF16),
            pltpu.VMEM(diag.shape, BF16),
            pltpu.VMEM(hops.shape, BF16),
            pltpu.VMEM((CHUNKS,) + piece, BF16),
            pltpu.VMEM((CHUNKS,) + piece, F32),
            pltpu.VMEM((exchanges, CHUNKS) + piece, BF16),
            pltpu.VMEM((exchanges, CHUNKS) + piece, BF16),
            pltpu.VMEM((exchanges, CHUNKS) + piece, BF16),
            pltpu.VMEM((exchanges, CHUNKS) + piece[1:], BF16),
            pltpu.VMEM((exchanges, CHUNKS) + piece[1:], BF16),
            dma((len(BLOCKS), times, sites)),
            dma((times, sites)),
            dma(()),
            dma(()),
            per_chunk, per_chunk, per_chunk, per_chunk,
            per_chunk, per_chunk, per_chunk, per_chunk,
            pltpu.SemaphoreType.REGULAR,
            pltpu.SemaphoreType.REGULAR,
        ],
        compiler_params=pltpu.CompilerParams(collective_id=0, has_side_effects=True, vmem_limit_bytes=grant),
        name="sweeps",
    )(fine, basis, diag, hops, table.T, agg)
    cells = pltpu.with_memory_space_constraint(cells, pltpu.VMEM)
    basis = pltpu.with_memory_space_constraint(basis, pltpu.VMEM)
    head = pltpu.with_memory_space_constraint(head, pltpu.VMEM)
    top = HEAD * rows
    return pl.pallas_call(
        prolong_kernel,
        out_shape=jax.ShapeDtypeStruct(fine.shape, BF16),
        in_specs=[vmem_spec] * 3,
        out_specs=any_spec,
        scratch_shapes=[
            pltpu.VMEM((times, sites, sources - top, depth), BF16),
            dma((times, sites)),
            dma((times, sites)),
        ],
        compiler_params=pltpu.CompilerParams(vmem_limit_bytes=grant),
        name="prolong",
    )(cells, basis, head)


def solution(mesh):
    return jax.shard_map(
        functools.partial(body, mesh.shape["lat"], mesh.shape["src"]),
        mesh=mesh,
        in_specs=(
            P("lat", "src", None, None),
            P("lat", "src", None, None),
            P("lat", "src", None, None),
            P("lat", "src", None, None, None),
            P(),
            P("lat", "src"),
        ),
        out_specs=P("lat", "src", None, None),
        check_vma=False,
    )
```

```python
import functools
import math

import jax
import jax.numpy as jnp
from jax import lax
from jax.experimental import pallas as pl
from jax.experimental.pallas import tpu as pltpu
from jax.sharding import PartitionSpec as P

SWEEPS = 3
DAMPING = 0.8
SIZES = (2, 2, 2, 2)
UNITS = sum(SIZES)
CHUNKS = len(SIZES)
BLOCKS = (1, 1, 2)
VMEM_BYTES = 67043328
DIRECT = 2
CROSS_BLOCK = 1
HEAD = 2
LAG = (3.8, 2.8)
SHIFT = 10.0
F32 = jnp.float32
BF16 = jnp.bfloat16


def dot(a, b):
    return jnp.dot(a, b, preferred_element_type=F32)


def first_unit(c):
    return sum(SIZES[:c])


def timetable(times, sites):
    steps = []
    for c in range(CHUNKS):
        end = first_unit(c + 1)
        for x in range(SWEEPS - 1):
            forward = end + SHIFT * x
            finish = forward + SIZES[c] + LAG[x]
            steps.append((forward, 0, "forward", x, c))
            steps.append((finish, 2, "finish", x, c))
            if x == 0:
                steps.append((end - 4.0, 1, "local", 0, c))
            if x + 1 < SWEEPS - 1:
                steps.append((finish + 0.2, 1, "local", x + 1, c))
            if x == SWEEPS - 2 and c == HEAD - 1:
                ready = finish
    count = times * sites
    for n in range(count):
        steps.append((ready + n * (UNITS - first_unit(HEAD)) / count, 3, "prolong", n // sites, n % sites))
    return [step[2:] for step in sorted(steps)]


def sweep_kernel(
    lats, srcs, fine, basis, diag, hops, table_h, agg_h, last, basis_v, out_v,
    table, agg, table_sem, agg_sem, fine_v, diag_v, hops_v, rhs, acc, cells, from_partner, from_far, above, below,
    fine_sem, basis_sem, diag_sem, hops_sem,
    partner_send, partner_recv, far_send, far_recv, above_send, above_recv, below_send, below_recv,
    direct_send, far_ready, cross_ready,
):
    times, sites, sources, _ = fine.shape
    width = basis.shape[3]
    rows = sources // UNITS
    lat, src = lax.axis_index("lat"), lax.axis_index("src")
    later, earlier = lax.rem(lat + 1, lats), lax.rem(lat + lats - 1, lats)
    odd = lax.rem(src, 2)
    partner = src + 1 - 2 * odd
    far_target = lax.rem(src + 2 - 4 * odd + srcs, srcs)
    mate = lat + 1 - 2 * lax.rem(lat, 2)
    cross = lax.rem(lat - 1 + 2 * lax.rem(lat, 2) + lats, lats)
    up, down = lax.rem(src + 2, srcs), lax.rem(src - 2 + srcs, srcs)
    first_of_cross = lat < cross
    barrier = pltpu.get_barrier_semaphore()

    def signal(semaphore, device):
        pl.semaphore_signal(semaphore, inc=1, device_id=device, device_id_type=pl.DeviceIdType.MESH)

    signal(barrier, (lat, down))
    signal(barrier, (lat, partner))
    signal(barrier, (mate, src))

    def meet():
        pl.semaphore_wait(barrier, jnp.where(first_of_cross, 3, 4))

        @pl.when(odd == 1)
        def _():
            signal(far_ready, (lat, up))

        @pl.when(jnp.logical_not(first_of_cross))
        def _():
            signal(cross_ready, (cross, src))

    spans = []
    for b, n in enumerate(BLOCKS):
        start = sum(BLOCKS[:b])
        spans.append((start, n, pl.ds(first_unit(start) * rows, sum(SIZES[start:start + n]) * rows)))

    def load_fine(b, t, s):
        span = spans[b][2]
        return pltpu.make_async_copy(fine.at[t, s, span], fine_v.at[t, s, span], fine_sem.at[b, t, s])

    def load_basis(t, s):
        return pltpu.make_async_copy(basis.at[t, s], basis_v.at[t, s], basis_sem.at[t, s])

    load_table = pltpu.make_async_copy(table_h, table, table_sem)
    load_agg = pltpu.make_async_copy(agg_h, agg, agg_sem)
    load_diag = pltpu.make_async_copy(diag, diag_v, diag_sem)
    load_hops = pltpu.make_async_copy(hops, hops_v, hops_sem)

    def start_block(b):
        for t in range(times):
            for s in range(sites):
                if b == 0:
                    load_basis(t, s).start()
                load_fine(b, t, s).start()
            if b == 0 and t == 0:
                load_diag.start()

    start_block(0)
    load_agg.start()
    load_table.start()

    @pl.when(first_of_cross)
    def _():
        signal(barrier, (cross, src))

    for b in range(1, len(BLOCKS)):
        start_block(b)
        if b == 1:
            load_hops.start()

    def remote(source, target, send, recv, device):
        return pltpu.make_async_remote_copy(
            src_ref=source, dst_ref=target, send_sem=send, recv_sem=recv,
            device_id=device, device_id_type=pl.DeviceIdType.MESH)

    def units(c):
        return pl.ds(first_unit(c), SIZES[c])

    def to_partner(x, c):
        return remote(cells.at[x, units(c)], from_partner.at[x, units(c)],
                      partner_send.at[x, c], partner_recv.at[x, c], (lat, partner))

    def to_far(x, c):
        return remote(from_partner.at[x, units(c)], from_far.at[x, units(c)],
                      far_send.at[x, c], far_recv.at[x, c], (lat, far_target))

    relays = far_target != 0
    is_last = src == srcs - 1

    def to_first(x, c):
        return remote(cells.at[x, units(c)], from_far.at[x, units(c)],
                      direct_send.at[x, c], far_recv.at[x, c], (lat, 0))

    def direct(x, c):
        return x == SWEEPS - 2 and c >= CHUNKS - DIRECT

    def to_later(x, c):
        return remote(cells.at[x, units(c), times - 1], below.at[x, units(c)],
                      below_send.at[x, c], below_recv.at[x, c], (later, src))

    def to_earlier(x, c):
        return remote(cells.at[x, units(c), 0], above.at[x, units(c)],
                      above_send.at[x, c], above_recv.at[x, c], (earlier, src))

    def send_time(x, c):
        to_later(x, c).start()
        to_earlier(x, c).start()

    def exchanged(t, values):
        swap = lax.rem(agg[t, 0], sites) == 1
        return [jnp.where(swap, values[1 - s], values[s]) for s in range(sites)]

    def restrict(b):
        first, n, span = spans[b]
        for t in range(times):
            for s in range(sites):
                if b == 0:
                    load_basis(t, s).wait()
                load_fine(b, t, s).wait()
        if b == 0:
            load_diag.wait()
            load_agg.wait()
        coarse = [[dot(fine_v[t, s, span], basis_v[t, s]) for s in range(sites)] for t in range(times)]
        here = [exchanged(t, [value.astype(BF16) for value in coarse[t]]) for t in range(times)]
        applied = [[dot(here[t][s], diag_v[t, s]) for s in range(sites)] for t in range(times)]
        for t in range(times):
            for s in range(sites):
                start = (DAMPING * applied[t][s]).astype(BF16)
                at = pl.ds(first_unit(first), sum(SIZES[first:first + n]))
                cells[0, at, t, s] = start.reshape(-1, rows, width)
                rhs[at, t, s] = here[t][s].reshape(-1, rows, width)
        if b == 0:
            meet()
        for i in range(n):
            to_partner(0, first + i).start()

    sent = 0
    for b in range(len(BLOCKS)):
        restrict(b)
        if b == CROSS_BLOCK:

            @pl.when(first_of_cross)
            def _():
                pl.semaphore_wait(cross_ready, 1)

        if b >= CROSS_BLOCK:
            done = spans[b][0] + spans[b][1]
            for c in range(sent, done):
                send_time(0, c)
            sent = done
    load_table.wait()
    load_hops.wait()

    partner_first = [table[0, src * sites + s] == partner * sites + s for s in range(sites)]

    def flat(value):
        return value.reshape(-1, width)

    def local(x, c):
        at = units(c)
        for t in range(times):
            for s in range(sites):
                own, other = flat(cells[x, at, t, s]), flat(cells[x, at, t, 1 - s])
                total = dot(jnp.concatenate([own, own], axis=1), hops_v[t, s, 2:4].reshape(-1, width))
                total += dot(jnp.concatenate([other, other], axis=1), hops_v[t, s, 4:6].reshape(-1, width))
                if t + 1 < times:
                    total += dot(flat(cells[x, at, t + 1, s]), hops_v[t, s, 6])
                if t > 0:
                    total += dot(flat(cells[x, at, t - 1, s]), hops_v[t, s, 7])
                acc[at, t, s] = (flat(rhs[at, t, s]).astype(F32) - total).reshape(-1, rows, width)

    def forward(x, c):
        to_partner(x, c).wait_recv()
        if x == 0 and c == 0:

            @pl.when(odd == 1)
            def _():
                pl.semaphore_wait(far_ready, 1)

        if direct(x, c):
            pl.when(relays)(lambda: to_far(x, c).start())
        else:
            to_far(x, c).start()

    def finish(x, c):
        to_earlier(x, c).wait_recv()
        to_later(x, c).wait_recv()
        to_far(x, c).wait_recv()
        at = units(c)
        blocks = [(t, s) for t in range(times) for s in range(sites)]
        totals = {}
        for t, s in blocks:
            near, far = flat(from_partner[x, at, t, s]), flat(from_far[x, at, t, s])
            pair = jnp.concatenate(
                [jnp.where(partner_first[s], near, far), jnp.where(partner_first[s], far, near)], axis=1)
            totals[t, s] = dot(pair, hops_v[t, s, 0:2].reshape(-1, width))
            if t == times - 1:
                totals[t, s] += dot(flat(above[x, at, s]), hops_v[t, s, 6])
            if t == 0:
                totals[t, s] += dot(flat(below[x, at, s]), hops_v[t, s, 7])
        differences = {(t, s): (flat(acc[at, t, s]) - totals[t, s]).astype(BF16) for t, s in blocks}
        applied = {(t, s): dot(differences[t, s], diag_v[t, s]) for t, s in blocks}
        new = {
            (t, s): ((1.0 - DAMPING) * flat(cells[x, at, t, s]).astype(F32) + DAMPING * applied[t, s]).astype(BF16)
            for t, s in blocks
        }
        if x + 1 < SWEEPS - 1:
            for t in range(times):
                for s in range(sites):
                    cells[x + 1, at, t, s] = new[t, s].reshape(-1, rows, width)
            if direct(x + 1, c):
                pl.when(is_last)(lambda: to_first(x + 1, c).start())
            to_partner(x + 1, c).start()
            send_time(x + 1, c)
        else:
            for t in range(times):
                gathered = exchanged(t, [new[t, s] for s in range(sites)])
                for s in range(sites):
                    last[t, s, pl.ds(first_unit(c) * rows, SIZES[c] * rows)] = gathered[s]

    def prolong(t, s):
        span = pl.ds(0, first_unit(HEAD) * rows)
        out_v[t, s, span] = lax.dot_general(
            last[t, s, span], basis_v[t, s], (((1,), (1,)), ((), ())), preferred_element_type=F32).astype(BF16)

    actions = {"forward": forward, "local": local, "finish": finish, "prolong": prolong}
    for name, *at in timetable(times, sites):
        actions[name](*at)

    for c in range(CHUNKS):
        for x in range(SWEEPS - 1):
            to_partner(x, c).wait_send()
            if direct(x, c):
                pl.when(relays)(lambda: to_far(x, c).wait_send())
                pl.when(is_last)(lambda: to_first(x, c).wait_send())
            else:
                to_far(x, c).wait_send()
            to_later(x, c).wait_send()
            to_earlier(x, c).wait_send()


def prolong_kernel(cells, basis, head_v, out, tail_v, head_sem, tail_sem):
    times, sites, sources, _ = cells.shape
    top = first_unit(HEAD) * (sources // UNITS)
    head, tail = pl.ds(0, top), pl.ds(top, sources - top)
    blocks = [(t, s) for t in range(times) for s in range(sites)]

    def store_head(t, s):
        return pltpu.make_async_copy(head_v.at[t, s, head], out.at[t, s, head], head_sem.at[t, s])

    def store_tail(t, s):
        return pltpu.make_async_copy(tail_v.at[t, s], out.at[t, s, tail], tail_sem.at[t, s])

    for t, s in blocks:
        store_head(t, s).start()
    for t, s in blocks:
        tail_v[t, s] = lax.dot_general(
            cells[t, s, tail], basis[t, s], (((1,), (1,)), ((), ())), preferred_element_type=F32).astype(BF16)
        store_tail(t, s).start()
    for t, s in blocks:
        store_head(t, s).wait()
        store_tail(t, s).wait()


def body(lats, srcs, fine, basis, diag, hops, table, agg):
    times, sites, sources, depth = fine.shape
    width = basis.shape[3]
    exchanges = SWEEPS - 1
    rows = sources // UNITS
    any_spec = pl.BlockSpec(memory_space=pl.ANY)
    vmem_spec = pl.BlockSpec(memory_space=pltpu.VMEM)
    dma = pltpu.SemaphoreType.DMA
    piece = (times, sites, rows, width)
    per_chunk = dma((exchanges, CHUNKS))
    handed = 2 * (times * sites * sources * width + math.prod(basis.shape) + math.prod(fine.shape))
    grant = VMEM_BYTES - handed - 2**18
    cells, basis, head = pl.pallas_call(
        functools.partial(sweep_kernel, lats, srcs),
        out_shape=[
            pltpu.VMEM((times, sites, sources, width), BF16),
            pltpu.VMEM(basis.shape, BF16),
            pltpu.VMEM(fine.shape, BF16),
        ],
        in_specs=[any_spec] * 6,
        out_specs=[vmem_spec] * 3,
        scratch_shapes=[
            pltpu.SMEM(table.shape[::-1], jnp.int32),
            pltpu.SMEM(agg.shape, jnp.int32),
            dma(()),
            dma(()),
            pltpu.VMEM(fine.shape, BF16),
            pltpu.VMEM(diag.shape, BF16),
            pltpu.VMEM(hops.shape, BF16),
            pltpu.VMEM((UNITS,) + piece, BF16),
            pltpu.VMEM((UNITS,) + piece, F32),
            pltpu.VMEM((exchanges, UNITS) + piece, BF16),
            pltpu.VMEM((exchanges, UNITS) + piece, BF16),
            pltpu.VMEM((exchanges, UNITS) + piece, BF16),
            pltpu.VMEM((exchanges, UNITS) + piece[1:], BF16),
            pltpu.VMEM((exchanges, UNITS) + piece[1:], BF16),
            dma((len(BLOCKS), times, sites)),
            dma((times, sites)),
            dma(()),
            dma(()),
            per_chunk, per_chunk, per_chunk, per_chunk,
            per_chunk, per_chunk, per_chunk, per_chunk,
            dma((exchanges, CHUNKS)),
            pltpu.SemaphoreType.REGULAR,
            pltpu.SemaphoreType.REGULAR,
        ],
        compiler_params=pltpu.CompilerParams(collective_id=0, has_side_effects=True, vmem_limit_bytes=grant),
        name="sweeps",
    )(fine, basis, diag, hops, table.T, agg)
    cells = pltpu.with_memory_space_constraint(cells, pltpu.VMEM)
    basis = pltpu.with_memory_space_constraint(basis, pltpu.VMEM)
    head = pltpu.with_memory_space_constraint(head, pltpu.VMEM)
    top = first_unit(HEAD) * rows
    return pl.pallas_call(
        prolong_kernel,
        out_shape=jax.ShapeDtypeStruct(fine.shape, BF16),
        in_specs=[vmem_spec] * 3,
        out_specs=any_spec,
        scratch_shapes=[
            pltpu.VMEM((times, sites, sources - top, depth), BF16),
            dma((times, sites)),
            dma((times, sites)),
        ],
        compiler_params=pltpu.CompilerParams(vmem_limit_bytes=grant),
        name="prolong",
    )(cells, basis, head)


def solution(mesh):
    return jax.shard_map(
        functools.partial(body, mesh.shape["lat"], mesh.shape["src"]),
        mesh=mesh,
        in_specs=(
            P("lat", "src", None, None),
            P("lat", "src", None, None),
            P("lat", "src", None, None),
            P("lat", "src", None, None, None),
            P(),
            P("lat", "src"),
        ),
        out_specs=P("lat", "src", None, None),
        check_vma=False,
    )
```

```python
import functools
import math

import jax
import jax.numpy as jnp
from jax import lax
from jax.experimental import pallas as pl
from jax.experimental.pallas import tpu as pltpu
from jax.sharding import PartitionSpec as P

SWEEPS = 3
DAMPING = 0.8
SIZES = (2, 2, 2, 2)
UNITS = sum(SIZES)
CHUNKS = len(SIZES)
BLOCKS = (1, 1, 2)
VMEM_BYTES = 67043328
DIRECT = 2
CROSS_BLOCK = 1
HEAD = 2
LAG = (2.8, 2.8)
SHIFT = 10.0
F32 = jnp.float32
BF16 = jnp.bfloat16


def dot(a, b):
    return jnp.dot(a, b, preferred_element_type=F32)


def first_unit(c):
    return sum(SIZES[:c])


def timetable(times, sites):
    steps = []
    for c in range(CHUNKS):
        end = first_unit(c + 1)
        for x in range(SWEEPS - 1):
            forward = end + SHIFT * x
            finish = forward + SIZES[c] + LAG[x]
            steps.append((forward, 0, "forward", x, c))
            steps.append((finish, 2, "finish", x, c))
            if x == 0:
                steps.append((end - 4.0, 1, "local", 0, c))
            if x + 1 < SWEEPS - 1:
                steps.append((finish + 0.2, 1, "local", x + 1, c))
            if x == SWEEPS - 2 and c == HEAD - 1:
                ready = finish
    count = times * sites
    for n in range(count):
        steps.append((ready + n * (UNITS - first_unit(HEAD)) / count, 3, "prolong", n // sites, n % sites))
    return [step[2:] for step in sorted(steps)]


def sweep_kernel(
    lats, srcs, fine, basis, diag, hops, table_h, agg_h, last, basis_v, out_v,
    table, agg, table_sem, agg_sem, fine_v, diag_v, hops_v, rhs, acc, remote_v, cells, from_partner, from_far, above, below,
    fine_sem, basis_sem, diag_sem, hops_sem,
    partner_send, partner_recv, far_send, far_recv, above_send, above_recv, below_send, below_recv,
    direct_send, far_ready, cross_ready,
):
    times, sites, sources, _ = fine.shape
    width = basis.shape[3]
    rows = sources // UNITS
    lat, src = lax.axis_index("lat"), lax.axis_index("src")
    later, earlier = lax.rem(lat + 1, lats), lax.rem(lat + lats - 1, lats)
    odd = lax.rem(src, 2)
    partner = src + 1 - 2 * odd
    far_target = lax.rem(src + 2 - 4 * odd + srcs, srcs)
    mate = lat + 1 - 2 * lax.rem(lat, 2)
    cross = lax.rem(lat - 1 + 2 * lax.rem(lat, 2) + lats, lats)
    up, down = lax.rem(src + 2, srcs), lax.rem(src - 2 + srcs, srcs)
    first_of_cross = lat < cross
    barrier = pltpu.get_barrier_semaphore()

    def signal(semaphore, device):
        pl.semaphore_signal(semaphore, inc=1, device_id=device, device_id_type=pl.DeviceIdType.MESH)

    signal(barrier, (lat, down))
    signal(barrier, (lat, partner))
    signal(barrier, (mate, src))

    def meet():
        pl.semaphore_wait(barrier, jnp.where(first_of_cross, 3, 4))

        @pl.when(odd == 1)
        def _():
            signal(far_ready, (lat, up))

        @pl.when(jnp.logical_not(first_of_cross))
        def _():
            signal(cross_ready, (cross, src))

    spans = []
    for b, n in enumerate(BLOCKS):
        start = sum(BLOCKS[:b])
        spans.append((start, n, pl.ds(first_unit(start) * rows, sum(SIZES[start:start + n]) * rows)))

    def load_fine(b, t, s):
        span = spans[b][2]
        return pltpu.make_async_copy(fine.at[t, s, span], fine_v.at[t, s, span], fine_sem.at[b, t, s])

    def load_basis(t, s):
        return pltpu.make_async_copy(basis.at[t, s], basis_v.at[t, s], basis_sem.at[t, s])

    load_table = pltpu.make_async_copy(table_h, table, table_sem)
    load_agg = pltpu.make_async_copy(agg_h, agg, agg_sem)
    load_diag = pltpu.make_async_copy(diag, diag_v, diag_sem)
    load_hops = pltpu.make_async_copy(hops, hops_v, hops_sem)

    def start_block(b):
        for t in range(times):
            for s in range(sites):
                if b == 0:
                    load_basis(t, s).start()
                load_fine(b, t, s).start()
            if b == 0 and t == 0:
                load_diag.start()

    start_block(0)
    load_agg.start()
    load_table.start()

    @pl.when(first_of_cross)
    def _():
        signal(barrier, (cross, src))

    for b in range(1, len(BLOCKS)):
        start_block(b)
        if b == 1:
            load_hops.start()

    def remote(source, target, send, recv, device):
        return pltpu.make_async_remote_copy(
            src_ref=source, dst_ref=target, send_sem=send, recv_sem=recv,
            device_id=device, device_id_type=pl.DeviceIdType.MESH)

    def units(c):
        return pl.ds(first_unit(c), SIZES[c])

    def to_partner(x, c):
        return remote(cells.at[x, units(c)], from_partner.at[x, units(c)],
                      partner_send.at[x, c], partner_recv.at[x, c], (lat, partner))

    def to_far(x, c):
        return remote(from_partner.at[x, units(c)], from_far.at[x, units(c)],
                      far_send.at[x, c], far_recv.at[x, c], (lat, far_target))

    relays = far_target != 0
    is_last = src == srcs - 1

    def to_first(x, c):
        return remote(cells.at[x, units(c)], from_far.at[x, units(c)],
                      direct_send.at[x, c], far_recv.at[x, c], (lat, 0))

    def direct(x, c):
        return x == SWEEPS - 2 and c >= CHUNKS - DIRECT

    def to_later(x, c):
        return remote(cells.at[x, units(c), times - 1], below.at[x, units(c)],
                      below_send.at[x, c], below_recv.at[x, c], (later, src))

    def to_earlier(x, c):
        return remote(cells.at[x, units(c), 0], above.at[x, units(c)],
                      above_send.at[x, c], above_recv.at[x, c], (earlier, src))

    def send_time(x, c):
        to_later(x, c).start()
        to_earlier(x, c).start()

    def exchanged(t, values):
        swap = lax.rem(agg[t, 0], sites) == 1
        return [jnp.where(swap, values[1 - s], values[s]) for s in range(sites)]

    def restrict(b):
        first, n, span = spans[b]
        for t in range(times):
            for s in range(sites):
                if b == 0:
                    load_basis(t, s).wait()
                load_fine(b, t, s).wait()
        if b == 0:
            load_diag.wait()
            load_agg.wait()
        coarse = [[dot(fine_v[t, s, span], basis_v[t, s]) for s in range(sites)] for t in range(times)]
        here = [exchanged(t, [value.astype(BF16) for value in coarse[t]]) for t in range(times)]
        applied = [[dot(here[t][s], diag_v[t, s]) for s in range(sites)] for t in range(times)]
        for t in range(times):
            for s in range(sites):
                start = (DAMPING * applied[t][s]).astype(BF16)
                at = pl.ds(first_unit(first), sum(SIZES[first:first + n]))
                cells[0, at, t, s] = start.reshape(-1, rows, width)
                rhs[at, t, s] = here[t][s].reshape(-1, rows, width)
        if b == 0:
            meet()
        for i in range(n):
            to_partner(0, first + i).start()

    sent = 0
    for b in range(len(BLOCKS)):
        restrict(b)
        if b == CROSS_BLOCK:

            @pl.when(first_of_cross)
            def _():
                pl.semaphore_wait(cross_ready, 1)

        if b >= CROSS_BLOCK:
            done = spans[b][0] + spans[b][1]
            for c in range(sent, done):
                send_time(0, c)
            sent = done
    load_table.wait()
    load_hops.wait()

    partner_first = [table[0, src * sites + s] == partner * sites + s for s in range(sites)]

    def prepare():
        for t in range(times):
            for s in range(sites):
                own = diag_v[t, s]
                columns = [0, 1] + ([6] if t == times - 1 else []) + ([7] if t == 0 else [])
                for i, k in enumerate(columns):
                    remote_v[t, s, i] = (DAMPING * dot(hops_v[t, s, k], own)).astype(BF16)

    def flat(value):
        return value.reshape(-1, width)

    def local(x, c):
        at = units(c)
        blocks = [(t, s) for t in range(times) for s in range(sites)]
        totals = {}
        for t in range(times):
            for s in range(sites):
                own, other = flat(cells[x, at, t, s]), flat(cells[x, at, t, 1 - s])
                total = dot(jnp.concatenate([own, own], axis=1), hops_v[t, s, 2:4].reshape(-1, width))
                total += dot(jnp.concatenate([other, other], axis=1), hops_v[t, s, 4:6].reshape(-1, width))
                if t + 1 < times:
                    total += dot(flat(cells[x, at, t + 1, s]), hops_v[t, s, 6])
                if t > 0:
                    total += dot(flat(cells[x, at, t - 1, s]), hops_v[t, s, 7])
                totals[t, s] = (flat(rhs[at, t, s]).astype(F32) - total).astype(BF16)
        for t, s in blocks:
            applied = dot(totals[t, s], diag_v[t, s])
            kept = (1.0 - DAMPING) * flat(cells[x, at, t, s]).astype(F32) + DAMPING * applied
            acc[at, t, s] = kept.reshape(-1, rows, width)

    def forward(x, c):
        to_partner(x, c).wait_recv()
        if x == 0 and c == 0:

            @pl.when(odd == 1)
            def _():
                pl.semaphore_wait(far_ready, 1)

        if direct(x, c):
            pl.when(relays)(lambda: to_far(x, c).start())
        else:
            to_far(x, c).start()

    def finish(x, c):
        to_earlier(x, c).wait_recv()
        to_later(x, c).wait_recv()
        to_far(x, c).wait_recv()
        at = units(c)
        blocks = [(t, s) for t in range(times) for s in range(sites)]
        new = {}
        for t, s in blocks:
            near, far = flat(from_partner[x, at, t, s]), flat(from_far[x, at, t, s])
            pair = jnp.concatenate(
                [jnp.where(partner_first[s], near, far), jnp.where(partner_first[s], far, near)], axis=1)
            total = dot(pair, remote_v[t, s, 0:2].reshape(-1, width))
            i = 2
            if t == times - 1:
                total += dot(flat(above[x, at, s]), remote_v[t, s, i])
                i += 1
            if t == 0:
                total += dot(flat(below[x, at, s]), remote_v[t, s, i])
            new[t, s] = (flat(acc[at, t, s]) - total).astype(BF16)
        if x + 1 < SWEEPS - 1:
            for t in range(times):
                for s in range(sites):
                    cells[x + 1, at, t, s] = new[t, s].reshape(-1, rows, width)
            if direct(x + 1, c):
                pl.when(is_last)(lambda: to_first(x + 1, c).start())
            to_partner(x + 1, c).start()
            send_time(x + 1, c)
        else:
            for t in range(times):
                gathered = exchanged(t, [new[t, s] for s in range(sites)])
                for s in range(sites):
                    last[t, s, pl.ds(first_unit(c) * rows, SIZES[c] * rows)] = gathered[s]

    def prolong(t, s):
        span = pl.ds(0, first_unit(HEAD) * rows)
        out_v[t, s, span] = lax.dot_general(
            last[t, s, span], basis_v[t, s], (((1,), (1,)), ((), ())), preferred_element_type=F32).astype(BF16)

    actions = {"forward": forward, "local": local, "finish": finish, "prolong": prolong}
    prepare()
    for name, *at in timetable(times, sites):
        actions[name](*at)

    for c in range(CHUNKS):
        for x in range(SWEEPS - 1):
            to_partner(x, c).wait_send()
            if direct(x, c):
                pl.when(relays)(lambda: to_far(x, c).wait_send())
                pl.when(is_last)(lambda: to_first(x, c).wait_send())
            else:
                to_far(x, c).wait_send()
            to_later(x, c).wait_send()
            to_earlier(x, c).wait_send()


def prolong_kernel(cells, basis, head_v, out, tail_v, head_sem, tail_sem):
    times, sites, sources, _ = cells.shape
    top = first_unit(HEAD) * (sources // UNITS)
    head, tail = pl.ds(0, top), pl.ds(top, sources - top)
    blocks = [(t, s) for t in range(times) for s in range(sites)]

    def store_head(t, s):
        return pltpu.make_async_copy(head_v.at[t, s, head], out.at[t, s, head], head_sem.at[t, s])

    def store_tail(t, s):
        return pltpu.make_async_copy(tail_v.at[t, s], out.at[t, s, tail], tail_sem.at[t, s])

    for t, s in blocks:
        store_head(t, s).start()
    for t, s in blocks:
        tail_v[t, s] = lax.dot_general(
            cells[t, s, tail], basis[t, s], (((1,), (1,)), ((), ())), preferred_element_type=F32).astype(BF16)
        store_tail(t, s).start()
    for t, s in blocks:
        store_head(t, s).wait()
        store_tail(t, s).wait()


def body(lats, srcs, fine, basis, diag, hops, table, agg):
    times, sites, sources, depth = fine.shape
    width = basis.shape[3]
    exchanges = SWEEPS - 1
    rows = sources // UNITS
    any_spec = pl.BlockSpec(memory_space=pl.ANY)
    vmem_spec = pl.BlockSpec(memory_space=pltpu.VMEM)
    dma = pltpu.SemaphoreType.DMA
    piece = (times, sites, rows, width)
    per_chunk = dma((exchanges, CHUNKS))
    handed = 2 * (times * sites * sources * width + math.prod(basis.shape) + math.prod(fine.shape))
    grant = VMEM_BYTES - handed - 2**18
    cells, basis, head = pl.pallas_call(
        functools.partial(sweep_kernel, lats, srcs),
        out_shape=[
            pltpu.VMEM((times, sites, sources, width), BF16),
            pltpu.VMEM(basis.shape, BF16),
            pltpu.VMEM(fine.shape, BF16),
        ],
        in_specs=[any_spec] * 6,
        out_specs=[vmem_spec] * 3,
        scratch_shapes=[
            pltpu.SMEM(table.shape[::-1], jnp.int32),
            pltpu.SMEM(agg.shape, jnp.int32),
            dma(()),
            dma(()),
            pltpu.VMEM(fine.shape, BF16),
            pltpu.VMEM(diag.shape, BF16),
            pltpu.VMEM(hops.shape, BF16),
            pltpu.VMEM((UNITS,) + piece, BF16),
            pltpu.VMEM((UNITS,) + piece, F32),
            pltpu.VMEM(hops.shape[:2] + (4,) + hops.shape[3:], BF16),
            pltpu.VMEM((exchanges, UNITS) + piece, BF16),
            pltpu.VMEM((exchanges, UNITS) + piece, BF16),
            pltpu.VMEM((exchanges, UNITS) + piece, BF16),
            pltpu.VMEM((exchanges, UNITS) + piece[1:], BF16),
            pltpu.VMEM((exchanges, UNITS) + piece[1:], BF16),
            dma((len(BLOCKS), times, sites)),
            dma((times, sites)),
            dma(()),
            dma(()),
            per_chunk, per_chunk, per_chunk, per_chunk,
            per_chunk, per_chunk, per_chunk, per_chunk,
            dma((exchanges, CHUNKS)),
            pltpu.SemaphoreType.REGULAR,
            pltpu.SemaphoreType.REGULAR,
        ],
        compiler_params=pltpu.CompilerParams(collective_id=0, has_side_effects=True, vmem_limit_bytes=grant),
        name="sweeps",
    )(fine, basis, diag, hops, table.T, agg)
    cells = pltpu.with_memory_space_constraint(cells, pltpu.VMEM)
    basis = pltpu.with_memory_space_constraint(basis, pltpu.VMEM)
    head = pltpu.with_memory_space_constraint(head, pltpu.VMEM)
    top = first_unit(HEAD) * rows
    return pl.pallas_call(
        prolong_kernel,
        out_shape=jax.ShapeDtypeStruct(fine.shape, BF16),
        in_specs=[vmem_spec] * 3,
        out_specs=any_spec,
        scratch_shapes=[
            pltpu.VMEM((times, sites, sources - top, depth), BF16),
            dma((times, sites)),
            dma((times, sites)),
        ],
        compiler_params=pltpu.CompilerParams(vmem_limit_bytes=grant),
        name="prolong",
    )(cells, basis, head)


def solution(mesh):
    return jax.shard_map(
        functools.partial(body, mesh.shape["lat"], mesh.shape["src"]),
        mesh=mesh,
        in_specs=(
            P("lat", "src", None, None),
            P("lat", "src", None, None),
            P("lat", "src", None, None),
            P("lat", "src", None, None, None),
            P(),
            P("lat", "src"),
        ),
        out_specs=P("lat", "src", None, None),
        check_vma=False,
    )
```

```python
import functools
import math

import jax
import jax.numpy as jnp
from jax import lax
from jax.experimental import pallas as pl
from jax.experimental.pallas import tpu as pltpu
from jax.sharding import PartitionSpec as P

SWEEPS = 3
DAMPING = 0.8
SIZES = (2, 2, 2, 2)
UNITS = sum(SIZES)
CHUNKS = len(SIZES)
BLOCKS = (1, 1, 2)
VMEM_BYTES = 67043328
DIRECT = 2
CROSS_BLOCK = 1
HEAD = 2
LAG = (2.8, 2.8)
SHIFT = 9.0
F32 = jnp.float32
BF16 = jnp.bfloat16


def dot(a, b):
    return jnp.dot(a, b, preferred_element_type=F32)


def first_unit(c):
    return sum(SIZES[:c])


def timetable(times, sites):
    steps = []
    for c in range(CHUNKS):
        end = first_unit(c + 1)
        for x in range(SWEEPS - 1):
            forward = end + SHIFT * x
            finish = forward + SIZES[c] + LAG[x]
            steps.append((forward, 0, "forward", x, c))
            steps.append((finish, 2, "finish", x, c))
            if x == 0:
                steps.append((end - 4.0, 1, "local", 0, c))
            if x + 1 < SWEEPS - 1:
                steps.append((finish + 0.2, 1, "local", x + 1, c))
            if x == SWEEPS - 2 and c == HEAD - 1:
                ready = finish
    count = times * sites
    for n in range(count):
        steps.append((ready + n * (UNITS - first_unit(HEAD)) / count, 3, "prolong", n // sites, n % sites))
    return [step[2:] for step in sorted(steps)]


def sweep_kernel(
    lats, srcs, fine, basis, diag, hops, table_h, agg_h, last, basis_v, out_v,
    table, agg, table_sem, agg_sem, fine_v, diag_v, hops_v, rhs, acc, remote_v, cells, from_partner, from_far, above, below,
    fine_sem, basis_sem, diag_sem, hops_sem,
    partner_send, partner_recv, far_send, far_recv, above_send, above_recv, below_send, below_recv,
    direct_send, far_ready, cross_ready,
):
    times, sites, sources, _ = fine.shape
    width = basis.shape[3]
    rows = sources // UNITS
    lat, src = lax.axis_index("lat"), lax.axis_index("src")
    later, earlier = lax.rem(lat + 1, lats), lax.rem(lat + lats - 1, lats)
    odd = lax.rem(src, 2)
    partner = src + 1 - 2 * odd
    far_target = lax.rem(src + 2 - 4 * odd + srcs, srcs)
    mate = lat + 1 - 2 * lax.rem(lat, 2)
    cross = lax.rem(lat - 1 + 2 * lax.rem(lat, 2) + lats, lats)
    up, down = lax.rem(src + 2, srcs), lax.rem(src - 2 + srcs, srcs)
    first_of_cross = lat < cross
    barrier = pltpu.get_barrier_semaphore()

    def signal(semaphore, device):
        pl.semaphore_signal(semaphore, inc=1, device_id=device, device_id_type=pl.DeviceIdType.MESH)

    signal(barrier, (lat, down))
    signal(barrier, (lat, partner))
    signal(barrier, (mate, src))

    def meet():
        pl.semaphore_wait(barrier, jnp.where(first_of_cross, 3, 4))

        @pl.when(odd == 1)
        def _():
            signal(far_ready, (lat, up))

        @pl.when(jnp.logical_not(first_of_cross))
        def _():
            signal(cross_ready, (cross, src))

    spans = []
    for b, n in enumerate(BLOCKS):
        start = sum(BLOCKS[:b])
        spans.append((start, n, pl.ds(first_unit(start) * rows, sum(SIZES[start:start + n]) * rows)))

    def load_fine(b, t, s):
        span = spans[b][2]
        return pltpu.make_async_copy(fine.at[t, s, span], fine_v.at[t, s, span], fine_sem.at[b, t, s])

    def load_basis(t, s):
        return pltpu.make_async_copy(basis.at[t, s], basis_v.at[t, s], basis_sem.at[t, s])

    load_table = pltpu.make_async_copy(table_h, table, table_sem)
    load_agg = pltpu.make_async_copy(agg_h, agg, agg_sem)
    load_diag = pltpu.make_async_copy(diag, diag_v, diag_sem)
    load_hops = pltpu.make_async_copy(hops, hops_v, hops_sem)

    def start_block(b):
        for t in range(times):
            for s in range(sites):
                if b == 0:
                    load_basis(t, s).start()
                load_fine(b, t, s).start()
            if b == 0 and t == 0:
                load_diag.start()

    start_block(0)
    load_agg.start()
    load_table.start()

    @pl.when(first_of_cross)
    def _():
        signal(barrier, (cross, src))

    for b in range(1, len(BLOCKS)):
        start_block(b)
        if b == 1:
            load_hops.start()

    def remote(source, target, send, recv, device):
        return pltpu.make_async_remote_copy(
            src_ref=source, dst_ref=target, send_sem=send, recv_sem=recv,
            device_id=device, device_id_type=pl.DeviceIdType.MESH)

    def units(c):
        return pl.ds(first_unit(c), SIZES[c])

    def to_partner(x, c):
        return remote(cells.at[x, units(c)], from_partner.at[x, units(c)],
                      partner_send.at[x, c], partner_recv.at[x, c], (lat, partner))

    def to_far(x, c):
        return remote(from_partner.at[x, units(c)], from_far.at[x, units(c)],
                      far_send.at[x, c], far_recv.at[x, c], (lat, far_target))

    relays = far_target != 0
    is_last = src == srcs - 1

    def to_first(x, c):
        return remote(cells.at[x, units(c)], from_far.at[x, units(c)],
                      direct_send.at[x, c], far_recv.at[x, c], (lat, 0))

    def direct(x, c):
        return x == SWEEPS - 2 and c >= CHUNKS - DIRECT

    def to_later(x, c):
        return remote(cells.at[x, units(c), times - 1], below.at[x, units(c)],
                      below_send.at[x, c], below_recv.at[x, c], (later, src))

    def to_earlier(x, c):
        return remote(cells.at[x, units(c), 0], above.at[x, units(c)],
                      above_send.at[x, c], above_recv.at[x, c], (earlier, src))

    def send_time(x, c):
        to_later(x, c).start()
        to_earlier(x, c).start()

    def exchanged(t, values):
        swap = lax.rem(agg[t, 0], sites) == 1
        return [jnp.where(swap, values[1 - s], values[s]) for s in range(sites)]

    def restrict(b):
        first, n, span = spans[b]
        for t in range(times):
            for s in range(sites):
                if b == 0:
                    load_basis(t, s).wait()
                load_fine(b, t, s).wait()
        if b == 0:
            load_diag.wait()
            load_agg.wait()
        coarse = [[dot(fine_v[t, s, span], basis_v[t, s]) for s in range(sites)] for t in range(times)]
        here = [exchanged(t, [value.astype(BF16) for value in coarse[t]]) for t in range(times)]
        applied = [[dot(here[t][s], diag_v[t, s]) for s in range(sites)] for t in range(times)]
        for t in range(times):
            for s in range(sites):
                start = (DAMPING * applied[t][s]).astype(BF16)
                at = pl.ds(first_unit(first), sum(SIZES[first:first + n]))
                cells[0, at, t, s] = start.reshape(-1, rows, width)
                rhs[at, t, s] = here[t][s].reshape(-1, rows, width)
        if b == 0:
            meet()
        for i in range(n):
            to_partner(0, first + i).start()

    sent = 0
    for b in range(len(BLOCKS)):
        restrict(b)
        if b == CROSS_BLOCK:

            @pl.when(first_of_cross)
            def _():
                pl.semaphore_wait(cross_ready, 1)

        if b >= CROSS_BLOCK:
            done = spans[b][0] + spans[b][1]
            for c in range(sent, done):
                send_time(0, c)
            sent = done
    load_table.wait()
    load_hops.wait()

    partner_first = [table[0, src * sites + s] == partner * sites + s for s in range(sites)]

    def prepare():
        for t in range(times):
            for s in range(sites):
                own = diag_v[t, s]
                columns = [0, 1] + ([6] if t == times - 1 else []) + ([7] if t == 0 else [])
                for i, k in enumerate(columns):
                    remote_v[t, s, i] = (DAMPING * dot(hops_v[t, s, k], own)).astype(BF16)

    def flat(value):
        return value.reshape(-1, width)

    def local(x, c):
        at = units(c)
        blocks = [(t, s) for t in range(times) for s in range(sites)]
        totals = {}
        for t in range(times):
            for s in range(sites):
                own, other = flat(cells[x, at, t, s]), flat(cells[x, at, t, 1 - s])
                total = dot(jnp.concatenate([own, own], axis=1), hops_v[t, s, 2:4].reshape(-1, width))
                total += dot(jnp.concatenate([other, other], axis=1), hops_v[t, s, 4:6].reshape(-1, width))
                if t + 1 < times:
                    total += dot(flat(cells[x, at, t + 1, s]), hops_v[t, s, 6])
                if t > 0:
                    total += dot(flat(cells[x, at, t - 1, s]), hops_v[t, s, 7])
                totals[t, s] = (flat(rhs[at, t, s]).astype(F32) - total).astype(BF16)
        for t, s in blocks:
            applied = dot(totals[t, s], diag_v[t, s])
            kept = (1.0 - DAMPING) * flat(cells[x, at, t, s]).astype(F32) + DAMPING * applied
            acc[at, t, s] = kept.reshape(-1, rows, width)

    def forward(x, c):
        to_partner(x, c).wait_recv()
        if x == 0 and c == 0:

            @pl.when(odd == 1)
            def _():
                pl.semaphore_wait(far_ready, 1)

        if direct(x, c):
            pl.when(relays)(lambda: to_far(x, c).start())
        else:
            to_far(x, c).start()

    def finish(x, c):
        to_earlier(x, c).wait_recv()
        to_later(x, c).wait_recv()
        to_far(x, c).wait_recv()
        at = units(c)
        blocks = [(t, s) for t in range(times) for s in range(sites)]
        new = {}
        for t, s in blocks:
            near, far = flat(from_partner[x, at, t, s]), flat(from_far[x, at, t, s])
            pair = jnp.concatenate(
                [jnp.where(partner_first[s], near, far), jnp.where(partner_first[s], far, near)], axis=1)
            total = dot(pair, remote_v[t, s, 0:2].reshape(-1, width))
            i = 2
            if t == times - 1:
                total += dot(flat(above[x, at, s]), remote_v[t, s, i])
                i += 1
            if t == 0:
                total += dot(flat(below[x, at, s]), remote_v[t, s, i])
            new[t, s] = (flat(acc[at, t, s]) - total).astype(BF16)
        if x + 1 < SWEEPS - 1:
            for t in range(times):
                for s in range(sites):
                    cells[x + 1, at, t, s] = new[t, s].reshape(-1, rows, width)
            if direct(x + 1, c):
                pl.when(is_last)(lambda: to_first(x + 1, c).start())
            to_partner(x + 1, c).start()
            send_time(x + 1, c)
        else:
            for t in range(times):
                gathered = exchanged(t, [new[t, s] for s in range(sites)])
                for s in range(sites):
                    last[t, s, pl.ds(first_unit(c) * rows, SIZES[c] * rows)] = gathered[s]

    def prolong(t, s):
        span = pl.ds(0, first_unit(HEAD) * rows)
        out_v[t, s, span] = lax.dot_general(
            last[t, s, span], basis_v[t, s], (((1,), (1,)), ((), ())), preferred_element_type=F32).astype(BF16)

    actions = {"forward": forward, "local": local, "finish": finish, "prolong": prolong}
    prepare()
    for name, *at in timetable(times, sites):
        actions[name](*at)

    for c in range(CHUNKS):
        for x in range(SWEEPS - 1):
            to_partner(x, c).wait_send()
            if direct(x, c):
                pl.when(relays)(lambda: to_far(x, c).wait_send())
                pl.when(is_last)(lambda: to_first(x, c).wait_send())
            else:
                to_far(x, c).wait_send()
            to_later(x, c).wait_send()
            to_earlier(x, c).wait_send()


def prolong_kernel(cells, basis, head_v, out, tail_v, head_sem, tail_sem):
    times, sites, sources, _ = cells.shape
    top = first_unit(HEAD) * (sources // UNITS)
    head, tail = pl.ds(0, top), pl.ds(top, sources - top)
    blocks = [(t, s) for t in range(times) for s in range(sites)]

    def store_head(t, s):
        return pltpu.make_async_copy(head_v.at[t, s, head], out.at[t, s, head], head_sem.at[t, s])

    def store_tail(t, s):
        return pltpu.make_async_copy(tail_v.at[t, s], out.at[t, s, tail], tail_sem.at[t, s])

    for t, s in blocks:
        store_head(t, s).start()
    for t, s in blocks:
        tail_v[t, s] = lax.dot_general(
            cells[t, s, tail], basis[t, s], (((1,), (1,)), ((), ())), preferred_element_type=F32).astype(BF16)
        store_tail(t, s).start()
    for t, s in blocks:
        store_head(t, s).wait()
        store_tail(t, s).wait()


def body(lats, srcs, fine, basis, diag, hops, table, agg):
    times, sites, sources, depth = fine.shape
    width = basis.shape[3]
    exchanges = SWEEPS - 1
    rows = sources // UNITS
    any_spec = pl.BlockSpec(memory_space=pl.ANY)
    vmem_spec = pl.BlockSpec(memory_space=pltpu.VMEM)
    dma = pltpu.SemaphoreType.DMA
    piece = (times, sites, rows, width)
    per_chunk = dma((exchanges, CHUNKS))
    handed = 2 * (times * sites * sources * width + math.prod(basis.shape) + math.prod(fine.shape))
    grant = VMEM_BYTES - handed - 2**18
    cells, basis, head = pl.pallas_call(
        functools.partial(sweep_kernel, lats, srcs),
        out_shape=[
            pltpu.VMEM((times, sites, sources, width), BF16),
            pltpu.VMEM(basis.shape, BF16),
            pltpu.VMEM(fine.shape, BF16),
        ],
        in_specs=[any_spec] * 6,
        out_specs=[vmem_spec] * 3,
        scratch_shapes=[
            pltpu.SMEM(table.shape[::-1], jnp.int32),
            pltpu.SMEM(agg.shape, jnp.int32),
            dma(()),
            dma(()),
            pltpu.VMEM(fine.shape, BF16),
            pltpu.VMEM(diag.shape, BF16),
            pltpu.VMEM(hops.shape, BF16),
            pltpu.VMEM((UNITS,) + piece, BF16),
            pltpu.VMEM((UNITS,) + piece, F32),
            pltpu.VMEM(hops.shape[:2] + (4,) + hops.shape[3:], BF16),
            pltpu.VMEM((exchanges, UNITS) + piece, BF16),
            pltpu.VMEM((exchanges, UNITS) + piece, BF16),
            pltpu.VMEM((exchanges, UNITS) + piece, BF16),
            pltpu.VMEM((exchanges, UNITS) + piece[1:], BF16),
            pltpu.VMEM((exchanges, UNITS) + piece[1:], BF16),
            dma((len(BLOCKS), times, sites)),
            dma((times, sites)),
            dma(()),
            dma(()),
            per_chunk, per_chunk, per_chunk, per_chunk,
            per_chunk, per_chunk, per_chunk, per_chunk,
            dma((exchanges, CHUNKS)),
            pltpu.SemaphoreType.REGULAR,
            pltpu.SemaphoreType.REGULAR,
        ],
        compiler_params=pltpu.CompilerParams(collective_id=0, has_side_effects=True, vmem_limit_bytes=grant),
        name="sweeps",
    )(fine, basis, diag, hops, table.T, agg)
    cells = pltpu.with_memory_space_constraint(cells, pltpu.VMEM)
    basis = pltpu.with_memory_space_constraint(basis, pltpu.VMEM)
    head = pltpu.with_memory_space_constraint(head, pltpu.VMEM)
    top = first_unit(HEAD) * rows
    return pl.pallas_call(
        prolong_kernel,
        out_shape=jax.ShapeDtypeStruct(fine.shape, BF16),
        in_specs=[vmem_spec] * 3,
        out_specs=any_spec,
        scratch_shapes=[
            pltpu.VMEM((times, sites, sources - top, depth), BF16),
            dma((times, sites)),
            dma((times, sites)),
        ],
        compiler_params=pltpu.CompilerParams(vmem_limit_bytes=grant),
        name="prolong",
    )(cells, basis, head)


def solution(mesh):
    return jax.shard_map(
        functools.partial(body, mesh.shape["lat"], mesh.shape["src"]),
        mesh=mesh,
        in_specs=(
            P("lat", "src", None, None),
            P("lat", "src", None, None),
            P("lat", "src", None, None),
            P("lat", "src", None, None, None),
            P(),
            P("lat", "src"),
        ),
        out_specs=P("lat", "src", None, None),
        check_vma=False,
    )
```
